512 devices in a mesh: grp: 16 (over y, core), mem: 32 (over x, z).
Axes of the slice: x: 4, y: 8, z: 8, core: 2. Of those that a mesh axis runs over, the one named last changes fastest.
Arguments:
- spectral: bfloat16 [512, 3, 2, 256, 192], P('grp', None, None, 'mem'), may hold values from -6 to 6
- inverse: bfloat16 [512, 192, 192], P('grp'), may hold values from -0.4375 to 0.4375
- legendre: bfloat16 [256, 256, 512], P('mem', None, 'grp'), may hold values from -0.015625 to 0.015625
- vorticity: bfloat16 [3, 256, 192, 1536], P(None, 'mem', 'grp'), may hold values from -6 to 6
- degree_list: int32 [512], replicated, may hold values from 0 to 511, as said below
- order_map: int32 [256], replicated, may hold values from 0 to 255, as said below
Outputs:
- advection: bfloat16 [3, 256, 192, 1536], P(None, 'mem', 'grp')
The draws below stay inside these ranges and needn't reach their ends.
Inputs may be any that keep to these rules, and one draw needn't show every extreme that they name: `degree_list`: a permutation of the degrees; slots 2j and 2j + 1 hold a degree d and 511 - d. `order_map`: a permutation of the orders; slots 2j and 2j + 1 hold an order m and 255 - m.
All inputs are finite; a program needn't handle non-finite values.
Results may differ from the reference program's by a relative error of at most 0.0062.
Values may be sent and summed in bfloat16 or wider, within the bound.
No kernel may reach another device: no remote copies, remote signals or barrier semaphores. Data moves between devices by JAX's collectives and lax.ppermute only.
A program may use at most 64 MiB of HBM per device.

```python
import math
import jax
import jax.numpy as jnp

L = 512
M = 256
R = 192
NPHI = 1536
NSH = 192
NLAT = 256


def paired_slots(key, count):
    lower = jax.random.permutation(key, count // 2).astype(jnp.int32)
    joined = jnp.stack([lower, count - 1 - lower], axis=1)
    return joined.reshape(count).astype(jnp.int32)


def draw_degree_list(key, part):
    return paired_slots(jax.random.fold_in(key, 11), L)


def draw_order_map(key, part):
    return paired_slots(jax.random.fold_in(key, 23), M)


def levels(key, dims, shards, smallest, high):
    factor_of = 1.0
    for dim, shards_of in shards:
        heights = jax.random.uniform(jax.random.fold_in(jax.random.fold_in(key, 6), dim), (shards_of,), jnp.float32, smallest / len(shards), high / len(shards))
        factor_of = factor_of * jnp.repeat(jnp.exp(heights), dims[dim] // shards_of).reshape((-1,) + (1,) * (len(dims) - 1 - dim))
    return factor_of


def noise(stream_key, shape, scale, bound, cuts=(), held_as=jnp.bfloat16):
    values = scale * jax.random.normal(stream_key, shape, jnp.float32)
    if cuts:
        values = values * levels(stream_key, shape, cuts, -0.22, 0.18)
    return jnp.clip(values, -bound, bound).astype(held_as)


def setup_inputs(seed: int = 0) -> dict:
    key_of = jax.random.split(jax.random.key(seed), 7)
    spectral = noise(key_of[0], (L, 3, 2, M, R), 1.0, 6.0, ((0, 16), (3, 32)))
    inverse = noise(key_of[1], (L, NSH, R), R ** -0.5, 0.4375, ((0, 16),))
    legendre = noise(key_of[2], (M, NLAT, L), (L * M) ** -0.5, 0.015625, ((0, 32), (2, 16)))
    vorticity = noise(key_of[3], (3, NLAT, NSH, NPHI), 1.0, 6.0, ((1, 32), (2, 16)))
    degree_list = draw_degree_list(jax.random.fold_in(key_of[6], 71), 0)
    order_map = draw_order_map(jax.random.fold_in(key_of[6], 71), 0)
    return dict(spectral=spectral, inverse=inverse, legendre=legendre, vorticity=vorticity, degree_list=degree_list, order_map=order_map)


def cross_product(flow_velocity, vorticity):
    other = vorticity.astype(jnp.float32)
    first = flow_velocity[:, :, 1] * other[2] - flow_velocity[:, :, 2] * other[1]
    second = flow_velocity[:, :, 2] * other[0] - flow_velocity[:, :, 0] * other[2]
    third = flow_velocity[:, :, 0] * other[1] - flow_velocity[:, :, 1] * other[0]
    return jnp.stack([first, second, third]).astype(jnp.bfloat16)


def fourier_table(order_map, count):
    longitude = jnp.arange(count, dtype=jnp.int32)
    phase = (order_map[:, None] * longitude[None, :]) % count
    angle = phase.astype(jnp.float32) * (2.0 * math.pi / count)
    weight = jnp.where(order_map == 0, 1.0, 2.0).astype(jnp.float32)[:, None]
    return jnp.stack([weight * jnp.cos(angle), -weight * jnp.sin(angle)], axis=1).astype(jnp.bfloat16)


def reference(spectral, inverse, legendre, vorticity, degree_list, order_map):
    valid = (degree_list[:, None] >= order_map[None, :]).astype(jnp.int32)
    radial_factor = jnp.einsum("agt,aefzt->agefz", inverse.astype(jnp.float32), spectral.astype(jnp.float32)).astype(jnp.bfloat16)
    table = legendre.astype(jnp.float32) * jnp.transpose(valid).astype(jnp.float32)[:, None, :]
    latitudinal = jnp.einsum("mtl,lsckm->mtsck", table, radial_factor.astype(jnp.float32)).astype(jnp.bfloat16)
    trig = fourier_table(order_map, NPHI)
    flow_velocity = jnp.einsum("mtsck,mkp->tscp", latitudinal.astype(jnp.float32), trig.astype(jnp.float32))
    return cross_product(flow_velocity, vorticity)
```

```python
import math

import jax
import jax.numpy as jnp
from jax import lax
from jax.experimental import pallas as pl
from jax.experimental.pallas import tpu as pltpu
from jax.sharding import Mesh
from jax.sharding import PartitionSpec as P

YS, YM, CORES = 2, 4, 2
CHIPS = YS * YM
F32, BF16 = jnp.float32, jnp.bfloat16


def dot(left, right, contract):
    return lax.dot_general(left, right, ((contract[:1], contract[1:]), ((), ())), preferred_element_type=F32)


def trig_tables(orders, count):
    longitude = jnp.arange(count, dtype=jnp.int32)
    phase = orders[:, None] * longitude[None, :] % count
    angle = phase.astype(F32) * (2.0 * math.pi / count)
    weight = jnp.where(orders == 0, 1.0, 2.0).astype(F32)[:, None]
    return (weight * jnp.cos(angle)).astype(BF16), (-weight * jnp.sin(angle)).astype(BF16)


def one_hot_rows(targets, width):
    return (targets[:, None] == jnp.arange(width, dtype=jnp.int32)[None, :]).astype(BF16)


def iota(shape, axis):
    return lax.broadcasted_iota(jnp.int32, shape, axis)


def pack_kernel(spec_ref, inv_ref, leg_ref, out_ref, solved_ref):
    degrees = spec_ref.shape[0]
    rows = degrees * 8
    for l in range(degrees):
        product = dot(spec_ref[l], inv_ref[l], (1, 1))
        for ck in range(6):
            solved_ref[ck, l * 8 : (l + 1) * 8, :] = product[ck * 8 : (ck + 1) * 8, :]
    r, c = iota((rows, rows), 0), iota((rows, rows), 1)
    swap = (c == r % degrees * 8 + r // degrees).astype(BF16)
    by_order = [dot(swap, solved_ref[ck].astype(BF16), (1, 0)) for ck in range(6)]
    half = by_order[0].shape[1] // YS
    for ys in range(YS):
        parts = [v[:, ys * half : (ys + 1) * half] for v in by_order]
        parts.append(jnp.zeros((rows, out_ref.shape[3] - 256 - 6 * half), F32))
        radial = jnp.concatenate(parts, axis=1).astype(BF16)
        for ym in range(YM):
            for o in range(2):
                at = (ym * 2 + o) * degrees
                out_ref[ys * YM + ym, o, :, 256:] = radial[at : at + degrees, :]
    r, c = iota((256, 256), 0), iota((256, 256), 1)
    turn = (r == c % 32 * 8 + c // 32).astype(BF16)
    table = dot(leg_ref[...].reshape(rows, 256), turn, (1, 0)).astype(BF16)
    for ym in range(YM):
        for o in range(2):
            at = (ym * 2 + o) * degrees
            for ys in range(YS):
                out_ref[ys * YM + ym, o, :, :256] = table[at : at + degrees, :]


def pack(spectral, inverse, legendre):
    degrees = spectral.shape[0]
    block = degrees // 2
    return pl.pallas_call(
        pack_kernel,
        out_shape=jax.ShapeDtypeStruct((CHIPS, 2, degrees, 896), BF16),
        grid=(2,),
        in_specs=[
            pl.BlockSpec((block, 48, 192), lambda i: (i, 0, 0)),
            pl.BlockSpec((block, 192, 192), lambda i: (i, 0, 0)),
            pl.BlockSpec((8, block, 256), lambda i: (0, i, 0)),
        ],
        out_specs=pl.BlockSpec((CHIPS, 2, block, 896), lambda i: (0, 0, i, 0)),
        scratch_shapes=[pltpu.VMEM((6, block * 8, 192), F32)],
        name="pack",
    )(spectral, inverse, legendre)


def contract_kernel(x_ref, valid_ref, place_ref, keep_ref, send_ref):
    for o in range(2):
        x = x_ref[:, o].reshape(256, 896)
        table = jnp.where(valid_ref[:, o : o + 1] > 0, x[:, :256], jnp.zeros((), BF16))
        values = dot(x[:, 256:], place_ref[...], (1, 0)).astype(BF16)
        partial = dot(table, values, (0, 0))
        keep_ref[o] = partial[:, :384]
        send_ref[o] = partial[:, 384:].astype(BF16)


def contract(received, valid, place):
    return pl.pallas_call(
        contract_kernel,
        out_shape=(
            jax.ShapeDtypeStruct((2, 256, 384), F32),
            jax.ShapeDtypeStruct((2, 256, 384), BF16),
        ),
        name="contract",
    )(received, valid, place)


def join_kernel(keep_ref, other_ref, out_ref):
    total = [(keep_ref[o] + other_ref[o].astype(F32)).astype(BF16).astype(F32) for o in range(2)]
    r, c = iota((64, 64), 0), iota((64, 64), 1)
    weave = (c == r % 2 * 32 + r // 2).astype(BF16)
    for ym in range(YM):
        halves = []
        for o in range(2):
            parts = [total[o][t * 32 : (t + 1) * 32, ym * 72 : (ym + 1) * 72] for t in range(8)]
            parts.append(jnp.zeros((32, 64), F32))
            halves.append(jnp.concatenate(parts, axis=1))
        pair = jnp.concatenate(halves, axis=0).astype(BF16)
        out_ref[ym * 64 : (ym + 1) * 64, :] = dot(weave, pair, (1, 0)).astype(BF16)


def join(keep, other):
    return pl.pallas_call(
        join_kernel, out_shape=jax.ShapeDtypeStruct((256, 640), BF16), name="join"
    )(keep, other)


def finish_kernel(x_ref, pick_ref, cos_ref, sin_ref, vort_ref, out_ref, lat_ref):
    @pl.when(pl.program_id(0) == 0)
    def _():
        for k in range(2):
            lat_ref[k] = dot(pick_ref[k], x_ref[...], (1, 1)).astype(BF16)

    flow = dot(lat_ref[0], cos_ref[...], (1, 0)) + dot(lat_ref[1], sin_ref[...], (1, 0))
    u = [flow[c * 96 : (c + 1) * 96] for c in range(3)]
    w = [vort_ref[c].astype(F32) for c in range(3)]
    for c in range(3):
        a, b = (c + 1) % 3, (c + 2) % 3
        out_ref[c] = (u[a] * w[b] - u[b] * w[a]).astype(BF16)


def finish(rows, pick, cos, sin, vorticity):
    width = 512
    return pl.pallas_call(
        finish_kernel,
        out_shape=jax.ShapeDtypeStruct(vorticity.shape, BF16),
        grid=(vorticity.shape[2] // width,),
        in_specs=[
            pl.BlockSpec((256, 640), lambda i: (0, 0)),
            pl.BlockSpec((2, 288, 640), lambda i: (0, 0, 0)),
            pl.BlockSpec((256, width), lambda i: (0, i)),
            pl.BlockSpec((256, width), lambda i: (0, i)),
            pl.BlockSpec((3, 96, width), lambda i: (0, 0, i)),
        ],
        out_specs=pl.BlockSpec((3, 96, width), lambda i: (0, 0, i)),
        scratch_shapes=[pltpu.VMEM((2, 288, 256), BF16)],
        name="finish",
    )(rows, pick, cos, sin, vorticity)


def shards(spectral, inverse, legendre, vorticity, degree_list, order_map):
    ym, core, mem = lax.axis_index("ym"), lax.axis_index("core"), lax.axis_index("mem")
    degrees = spectral.shape[0]
    packed = pack(
        spectral.reshape(degrees, 48, 192), inverse, jnp.transpose(legendre, (0, 2, 1))
    )
    received = lax.all_to_all(packed, ("ys", "ym"), 0, 0, tiled=True)

    orders = lax.dynamic_slice_in_dim(order_map, mem * 8 + ym * 2, 2)
    own = lax.dynamic_index_in_dim(degree_list.reshape(CHIPS, CORES, degrees), core, 1, False)
    valid = (own.reshape(-1)[:, None] >= orders[None, :]).astype(F32)
    col = jnp.arange(640, dtype=jnp.int32)
    ck, s = col // 96, col % 96
    side = jnp.where(s // 12 % 2 == core, 0, 384)
    target = jnp.where(col < 576, side + s // 24 * 72 + ck * 12 + s % 12, -1)
    keep, send = contract(received, valid, one_hot_rows(target, 768))

    other = lax.ppermute(send, "core", [(0, 1), (1, 0)])
    joined = join(keep, other)
    rows = lax.all_to_all(joined.reshape(128, 2, 640), ("ym", "mem"), 0, 0, tiled=True)

    row = jnp.arange(288, dtype=jnp.int32)
    base = row % 8 * 72 + row // 96 * 24 + row // 8 % 12
    pick = jnp.stack([one_hot_rows(base, 640), one_hot_rows(base + 12, 640)])
    member_orders = jnp.transpose(order_map.reshape(32, YM, 2), (1, 0, 2)).reshape(-1)
    cos, sin = trig_tables(member_orders, vorticity.shape[3])
    field = jnp.transpose(vorticity, (0, 2, 1, 3)).reshape(3, 96, vorticity.shape[3])
    out = finish(rows.reshape(256, 640), pick, cos, sin, field)
    return jnp.transpose(out.reshape(3, 12, 8, vorticity.shape[3]), (0, 2, 1, 3))


def solution(mesh):
    fine = Mesh(mesh.devices.reshape(YS, YM, CORES, 32), ("ys", "ym", "core", "mem"))
    grp = ("ys", "ym", "core")
    return jax.shard_map(
        shards,
        mesh=fine,
        in_specs=(
            P(grp, None, None, "mem", None),
            P(grp, None, None),
            P("mem", None, grp),
            P(None, "mem", grp, None),
            P(),
            P(),
        ),
        out_specs=P(None, "mem", grp, None),
        check_vma=False,
    )
```

```python
import math

import jax
import jax.numpy as jnp
from jax import lax
from jax.experimental import pallas as pl
from jax.experimental.pallas import tpu as pltpu
from jax.sharding import Mesh
from jax.sharding import PartitionSpec as P

YS, YM, CORES = 2, 4, 2
CHIPS = YS * YM
F32, BF16 = jnp.float32, jnp.bfloat16
STEPS = 4
PARAMS = pltpu.CompilerParams(vmem_limit_bytes=16 << 20)


def dot(left, right, contract):
    return lax.dot_general(left, right, ((contract[:1], contract[1:]), ((), ())), preferred_element_type=F32)


def iota(shape, axis):
    return lax.broadcasted_iota(jnp.int32, shape, axis)


def pack_kernel(spec_hbm, inv_hbm, leg_hbm, out_ref, spec_ref, inv_ref, leg_ref, solved_ref, sems):
    degrees = spec_ref.shape[0]
    rows = degrees * 8
    step = degrees // STEPS
    copies = []
    for i in range(STEPS):
        cut = pl.ds(i * step, step)
        copies.append(pltpu.make_async_copy(inv_hbm.at[cut], inv_ref.at[cut], sems.at[2 * i]))
        copies.append(pltpu.make_async_copy(spec_hbm.at[cut], spec_ref.at[cut], sems.at[2 * i + 1]))
    copies.append(pltpu.make_async_copy(leg_hbm, leg_ref, sems.at[2 * STEPS]))
    for copy in copies:
        copy.start()
    for i in range(STEPS):
        copies[2 * i].wait()
        copies[2 * i + 1].wait()
        for l in range(i * step, (i + 1) * step):
            product = dot(spec_ref[l], inv_ref[l], (1, 1))
            for ck in range(6):
                solved_ref[ck, l * 8 : (l + 1) * 8, :] = product[ck * 8 : (ck + 1) * 8, :]
    copies[-1].wait()
    r, c = iota((256, 256), 0), iota((256, 256), 1)
    turn = (r == c % 32 * 8 + c // 32).astype(BF16)
    table = dot(leg_ref[...].reshape(256, 256), turn, (1, 0)).astype(BF16)
    for chip in range(CHIPS):
        for o in range(2):
            at = (chip % YM * 2 + o) * degrees
            out_ref[chip, :, o * 256 : (o + 1) * 256] = table[at : at + degrees, :]
    r, c = iota((rows, rows), 0), iota((rows, rows), 1)
    swap = (c == r % degrees * 8 + r // degrees).astype(BF16)
    by_order = [dot(swap, solved_ref[ck].astype(BF16), (1, 0)) for ck in range(6)]
    half = by_order[0].shape[1] // YS
    for ys in range(YS):
        for ym in range(YM):
            parts = []
            for o in range(2):
                at = (ym * 2 + o) * degrees
                parts += [v[at : at + degrees, ys * half : (ys + 1) * half] for v in by_order]
            out_ref[ys * YM + ym, :, 512:] = jnp.concatenate(parts, axis=1).astype(BF16)


def pack(spectral, inverse, legendre):
    degrees = spectral.shape[0]
    return pl.pallas_call(
        pack_kernel,
        out_shape=jax.ShapeDtypeStruct((CHIPS, degrees, 1664), BF16),
        in_specs=[pl.BlockSpec(memory_space=pl.ANY)] * 3,
        scratch_shapes=[
            pltpu.VMEM(spectral.shape, BF16),
            pltpu.VMEM(inverse.shape, BF16),
            pltpu.VMEM(legendre.shape, BF16),
            pltpu.VMEM((6, degrees * 8, 192), F32),
            pltpu.SemaphoreType.DMA((2 * STEPS + 1,)),
        ],
        compiler_params=pltpu.CompilerParams(vmem_limit_bytes=60 << 20),
        name="pack",
    )(spectral, inverse, legendre)


def turned(values, index):
    hit = iota(index.shape, 1) == index
    return jnp.sum(jnp.where(hit, values, 0), axis=1, keepdims=True)


def tables_kernel(where_ref, order_ref, degree_ref, info_ref, place_ref, pick_ref, cos_ref, sin_ref):
    core, first = where_ref[0], where_ref[1]
    r = iota((256, 512), 0)
    own = turned(degree_ref[...].astype(F32), r // 32 * 64 + core * 32 + r % 32)
    orders = order_ref[...].astype(F32)
    for o in range(2):
        order = turned(orders, jnp.full((256, 256), first + o, jnp.int32))
        info_ref[:, o : o + 1] = (own >= order).astype(F32)
    q, col = iota((640, 768), 0), iota((640, 768), 1)
    ck, s = q // 96, q % 96
    side = jnp.where(s // 12 % 2 == core, 0, 384)
    hit = (col == side + s // 24 * 72 + ck * 12 + s % 12) & (q < 576)
    place_ref[...] = hit.astype(F32).astype(BF16)
    row, col = iota((288, 640), 0), iota((288, 640), 1)
    hit = col == row % 8 * 72 + row // 96 * 24 + row // 8 % 12
    pick_ref[...] = hit.astype(F32).astype(BF16)
    r = iota((256, 256), 0)
    order = turned(orders, r % 64 // 2 * 8 + r // 64 * 2 + r % 2)
    weight = jnp.where(order == 0, 1.0, 2.0)
    info_ref[:, 2:3] = 1.0 - 2.0 * (order - 2.0 * jnp.floor(order * 0.5))
    half = cos_ref.shape[1]
    count = 2 * half
    for at in range(0, half, 128):
        product = order * (iota((256, 128), 1) + at).astype(F32)
        phase = product - jnp.floor(product * (1.0 / count)) * count
        phase = jnp.where(phase < 0, phase + count, phase)
        phase = jnp.where(phase >= count, phase - count, phase)
        angle = phase * (2.0 * math.pi / count)
        cos_ref[:, at : at + 128] = (weight * jnp.cos(angle)).astype(BF16)
        sin_ref[:, at : at + 128] = (-weight * jnp.sin(angle)).astype(BF16)


def tables(where, order_map, degree_list, count):
    return pl.pallas_call(
        tables_kernel,
        out_shape=(
            jax.ShapeDtypeStruct((256, 3), F32),
            jax.ShapeDtypeStruct((640, 768), BF16),
            jax.ShapeDtypeStruct((288, 640), BF16),
            jax.ShapeDtypeStruct((256, count // 2), BF16),
            jax.ShapeDtypeStruct((256, count // 2), BF16),
        ),
        in_specs=[pl.BlockSpec(memory_space=pltpu.SMEM)]
        + [pl.BlockSpec(memory_space=pltpu.VMEM)] * 2,
        compiler_params=PARAMS,
        name="tables",
    )(where, order_map[None, :], degree_list[None, :])


def contract_kernel(x_ref, info_ref, place_ref, keep_ref, send_ref):
    for o in range(2):
        table = x_ref[:, :, o * 256 : (o + 1) * 256].reshape(256, 256)
        table = jnp.where(info_ref[:, o : o + 1] > 0, table, jnp.zeros((), BF16))
        radial = x_ref[:, :, 512 + o * 512 : 1152 + o * 512].reshape(256, 640)
        if o:
            radial = jnp.concatenate([radial[:, 64:], radial[:, :64]], axis=1)
        values = dot(radial, place_ref[...], (1, 0)).astype(BF16)
        partial = dot(table, values, (0, 0))
        keep_ref[o] = partial[:, :384]
        send_ref[o] = partial[:, 384:].astype(BF16)


def contract(received, info, place):
    return pl.pallas_call(
        contract_kernel,
        out_shape=(
            jax.ShapeDtypeStruct((2, 256, 384), F32),
            jax.ShapeDtypeStruct((2, 256, 384), BF16),
        ),
        compiler_params=PARAMS,
        name="contract",
    )(received, info, place)


def join_kernel(keep_ref, other_ref, out_ref):
    total = [(keep_ref[o] + other_ref[o].astype(F32)).astype(BF16).astype(F32) for o in range(2)]
    r, c = iota((64, 64), 0), iota((64, 64), 1)
    weave = (c == r % 2 * 32 + r // 2).astype(BF16)
    for ym in range(YM):
        halves = []
        for o in range(2):
            parts = [total[o][t * 32 : (t + 1) * 32, ym * 72 : (ym + 1) * 72] for t in range(8)]
            parts.append(jnp.zeros((32, 64), F32))
            halves.append(jnp.concatenate(parts, axis=1))
        pair = jnp.concatenate(halves, axis=0).astype(BF16)
        out_ref[ym * 64 : (ym + 1) * 64, :] = dot(weave, pair, (1, 0)).astype(BF16)


def join(keep, other):
    return pl.pallas_call(
        join_kernel,
        out_shape=jax.ShapeDtypeStruct((256, 640), BF16),
        compiler_params=PARAMS,
        name="join",
    )(keep, other)


def finish_kernel(x_ref, info_ref, pick_ref, cos_ref, sin_ref, vort_ref, out_ref, lat_ref):
    step = pl.program_id(0)
    side = step // (pl.num_programs(0) // 2)

    @pl.when(step == 0)
    def _():
        x = x_ref[...].astype(F32)
        x = jnp.concatenate([x, x * info_ref[:, 2:3]], axis=0)
        for k in range(2):
            turned_x = jnp.concatenate([x[:, 12:], x[:, :12]], axis=1) if k else x
            rows = dot(pick_ref[...], turned_x.astype(BF16), (1, 1)).astype(BF16)
            for h in range(2):
                lat_ref[h, k] = rows[:, h * 256 : (h + 1) * 256]

    flow = dot(lat_ref[side, 0], cos_ref[...], (1, 0)) + dot(lat_ref[side, 1], sin_ref[...], (1, 0))
    u = [flow[c * 96 : (c + 1) * 96] for c in range(3)]
    w = [vort_ref[c].astype(F32) for c in range(3)]
    for c in range(3):
        a, b = (c + 1) % 3, (c + 2) % 3
        out_ref[c] = (u[a] * w[b] - u[b] * w[a]).astype(BF16)


def finish(rows, info, pick, cos, sin, vorticity):
    width = 384
    blocks = cos.shape[1] // width
    return pl.pallas_call(
        finish_kernel,
        out_shape=jax.ShapeDtypeStruct(vorticity.shape, BF16),
        grid=(2 * blocks,),
        in_specs=[
            pl.BlockSpec((256, 640), lambda i: (0, 0)),
            pl.BlockSpec((256, 3), lambda i: (0, 0)),
            pl.BlockSpec((288, 640), lambda i: (0, 0)),
            pl.BlockSpec((256, width), lambda i: (0, i % blocks)),
            pl.BlockSpec((256, width), lambda i: (0, i % blocks)),
            pl.BlockSpec((3, 96, width), lambda i: (0, 0, i)),
        ],
        out_specs=pl.BlockSpec((3, 96, width), lambda i: (0, 0, i)),
        scratch_shapes=[pltpu.VMEM((2, 2, 288, 256), BF16)],
        compiler_params=PARAMS,
        name="finish",
    )(rows, info, pick, cos, sin, vorticity)


def shards(spectral, inverse, legendre, vorticity, degree_list, order_map):
    ym, core, mem = lax.axis_index("ym"), lax.axis_index("core"), lax.axis_index("mem")
    degrees = spectral.shape[0]
    packed = pack(
        spectral.reshape(degrees, 48, 192), inverse, jnp.transpose(legendre, (0, 2, 1))
    )
    received = lax.all_to_all(packed, ("ys", "ym"), 0, 0, tiled=True)
    where = jnp.stack([core, mem * 8 + ym * 2]).astype(jnp.int32)
    count = vorticity.shape[3]
    info, place, pick, cos, sin = tables(where, order_map, degree_list, count)
    keep, send = contract(received, info, place)
    other = lax.ppermute(send, "core", [(0, 1), (1, 0)])
    joined = join(keep, other)
    rows = lax.all_to_all(joined.reshape(128, 2, 640), ("ym", "mem"), 0, 0, tiled=True)

    field = jnp.transpose(vorticity, (0, 2, 1, 3)).reshape(3, 96, count)
    out = finish(rows.reshape(256, 640), info, pick, cos, sin, field)
    return jnp.transpose(out.reshape(3, 12, 8, count), (0, 2, 1, 3))


def solution(mesh):
    fine = Mesh(mesh.devices.reshape(YS, YM, CORES, 32), ("ys", "ym", "core", "mem"))
    grp = ("ys", "ym", "core")
    return jax.shard_map(
        shards,
        mesh=fine,
        in_specs=(
            P(grp, None, None, "mem", None),
            P(grp, None, None),
            P("mem", None, grp),
            P(None, "mem", grp, None),
            P(),
            P(),
        ),
        out_specs=P(None, "mem", grp, None),
        check_vma=False,
    )
```

```python
import math

import jax
import jax.numpy as jnp
from jax import lax
from jax.experimental import pallas as pl
from jax.experimental.pallas import tpu as pltpu
from jax.sharding import Mesh
from jax.sharding import PartitionSpec as P

YS, YM, CORES = 2, 4, 2
CHIPS = YS * YM
F32, BF16 = jnp.float32, jnp.bfloat16
STEPS = 4
WIDTH = 256
PARAMS = pltpu.CompilerParams(vmem_limit_bytes=16 << 20)


def dot(left, right, contract):
    return lax.dot_general(left, right, ((contract[:1], contract[1:]), ((), ())), preferred_element_type=F32)


def iota(shape, axis):
    return lax.broadcasted_iota(jnp.int32, shape, axis)


def pack_kernel(
    spec_hbm, inv_hbm, leg_hbm, out_hbm, out_ref, spec_ref, inv_ref, leg_ref, solved_ref, sems, out_sems
):
    degrees = spec_ref.shape[0]
    rows = degrees * 8
    step = degrees // STEPS
    copies = [pltpu.make_async_copy(leg_hbm, leg_ref, sems.at[2 * STEPS])]
    for i in range(STEPS):
        cut = pl.ds(i * step, step)
        copies.append(pltpu.make_async_copy(inv_hbm.at[cut], inv_ref.at[cut], sems.at[2 * i]))
        copies.append(pltpu.make_async_copy(spec_hbm.at[cut], spec_ref.at[cut], sems.at[2 * i + 1]))
    for copy in copies:
        copy.start()
    r, c = iota((256, 256), 0), iota((256, 256), 1)
    turn = (r == c % 32 * 8 + c // 32).astype(BF16)
    swap = (c == r % degrees * 8 + r // degrees).astype(BF16)
    copies[0].wait()
    table = dot(leg_ref[...].reshape(rows, 256), turn, (1, 0)).astype(BF16)
    for chip in range(CHIPS):
        for o in range(2):
            at = (chip % YM * 2 + o) * degrees
            out_ref[chip, :, o * 256 : (o + 1) * 256] = table[at : at + degrees, :]
    for i in range(STEPS):
        copies[2 * i + 1].wait()
        copies[2 * i + 2].wait()
        for l in range(i * step, (i + 1) * step):
            product = dot(spec_ref[l], inv_ref[l], (1, 1))
            for ck in range(6):
                solved_ref[ck, l * 8 : (l + 1) * 8, :] = product[ck * 8 : (ck + 1) * 8, :]
    r, c = iota((192, 192), 0), iota((192, 192), 1)
    side = (r // 12 % 2 != lax.axis_index("core")).astype(jnp.int32)
    near = (c == r // 96 * 96 + side * 48 + r % 96 // 24 * 12 + r % 12).astype(F32).astype(BF16)
    by_order = [dot(swap, solved_ref[ck].astype(BF16), (1, 0)).astype(BF16) for ck in range(6)]
    by_order = [dot(v, near, (1, 0)) for v in by_order]
    half = by_order[0].shape[1] // YS
    sends = []
    for ys in range(YS):
        for ym in range(YM):
            parts = []
            for o in range(2):
                at = (ym * 2 + o) * degrees
                parts += [v[at : at + degrees, ys * half : (ys + 1) * half] for v in by_order]
            chip = ys * YM + ym
            out_ref[chip, :, 512:] = jnp.concatenate(parts, axis=1).astype(BF16)
            sends.append(pltpu.make_async_copy(out_ref.at[chip], out_hbm.at[chip], out_sems.at[chip]))
            sends[-1].start()
    for send in sends:
        send.wait()


def pack(spectral, inverse, legendre):
    degrees = spectral.shape[0]
    return pl.pallas_call(
        pack_kernel,
        out_shape=jax.ShapeDtypeStruct((CHIPS, degrees, 1664), BF16),
        in_specs=[pl.BlockSpec(memory_space=pl.ANY)] * 3,
        out_specs=pl.BlockSpec(memory_space=pl.ANY),
        scratch_shapes=[
            pltpu.VMEM((CHIPS, degrees, 1664), BF16),
            pltpu.VMEM(spectral.shape, BF16),
            pltpu.VMEM(inverse.shape, BF16),
            pltpu.VMEM(legendre.shape, BF16),
            pltpu.VMEM((6, degrees * 8, 192), F32),
            pltpu.SemaphoreType.DMA((2 * STEPS + 1,)),
            pltpu.SemaphoreType.DMA((CHIPS,)),
        ],
        compiler_params=pltpu.CompilerParams(vmem_limit_bytes=60 << 20),
        name="pack",
    )(spectral, inverse, legendre)


def turned(values, index):
    hit = iota(index.shape, 1) == index
    return jnp.sum(jnp.where(hit, values, 0), axis=1, keepdims=True)


def tables_kernel(where_ref, order_ref, degree_ref, info_ref, place_ref, pick_ref, cos_ref, sin_ref):
    core, first = where_ref[0], where_ref[1]
    r = iota((256, 512), 0)
    own = turned(degree_ref[...].astype(F32), r // 32 * 64 + core * 32 + r % 32)
    orders = order_ref[...].astype(F32)
    for o in range(2):
        order = turned(orders, jnp.full((256, 256), first + o, jnp.int32))
        info_ref[:, o : o + 1] = (own >= order).astype(F32)
    q, col = iota((288, 384), 0), iota((288, 384), 1)
    hit = col == q % 48 // 12 * 72 + q // 48 * 12 + q % 12
    place_ref[...] = hit.astype(F32).astype(BF16)
    row, col = iota((288, 640), 0), iota((288, 640), 1)
    hit = col == row % 8 * 72 + row // 96 * 24 + row // 8 % 12
    pick_ref[...] = hit.astype(F32).astype(BF16)
    r = iota((256, 256), 0)
    order = turned(orders, r % 64 // 2 * 8 + r // 64 * 2 + r % 2)
    weight = jnp.where(order == 0, 1.0, 2.0)
    info_ref[:, 2:3] = 1.0 - 2.0 * (order - 2.0 * jnp.floor(order * 0.5))
    half = cos_ref.shape[1]
    count = 2 * half
    for at in range(0, half, 128):
        product = order * (iota((256, 128), 1) + at).astype(F32)
        phase = product - jnp.floor(product * (1.0 / count)) * count
        phase = jnp.where(phase < 0, phase + count, phase)
        phase = jnp.where(phase >= count, phase - count, phase)
        angle = phase * (2.0 * math.pi / count)
        cos_ref[:, at : at + 128] = (weight * jnp.cos(angle)).astype(BF16)
        sin_ref[:, at : at + 128] = (-weight * jnp.sin(angle)).astype(BF16)


def tables(where, order_map, degree_list, count):
    return pl.pallas_call(
        tables_kernel,
        out_shape=(
            jax.ShapeDtypeStruct((256, 3), F32),
            jax.ShapeDtypeStruct((288, 384), BF16),
            jax.ShapeDtypeStruct((288, 640), BF16),
            jax.ShapeDtypeStruct((256, count // 2), BF16),
            jax.ShapeDtypeStruct((256, count // 2), BF16),
        ),
        in_specs=[pl.BlockSpec(memory_space=pltpu.SMEM)]
        + [pl.BlockSpec(memory_space=pltpu.VMEM)] * 2,
        compiler_params=PARAMS,
        name="tables",
    )(where, order_map[None, :], degree_list[None, :])


def contract_kernel(x_ref, info_ref, keep_ref, send_ref):
    for o in range(2):
        table = x_ref[:, :, o * 256 : (o + 1) * 256].reshape(256, 256)
        table = jnp.where(info_ref[:, o : o + 1] > 0, table, jnp.zeros((), BF16))
        radial = x_ref[:, :, 512 + o * 512 : 1152 + o * 512].reshape(256, 640)
        partial = dot(radial, table, (0, 0))
        for ck in range(6):
            at = o * 64 + ck * 96
            keep_ref[o, ck * 48 : (ck + 1) * 48, :] = partial[at : at + 48, :]
            send_ref[o, ck * 48 : (ck + 1) * 48, :] = partial[at + 48 : at + 96, :].astype(BF16)


def contract(received, info):
    return pl.pallas_call(
        contract_kernel,
        out_shape=(
            jax.ShapeDtypeStruct((2, 288, 256), F32),
            jax.ShapeDtypeStruct((2, 288, 256), BF16),
        ),
        compiler_params=PARAMS,
        name="contract",
    )(received, info)


def join_kernel(keep_ref, other_ref, place_ref, out_ref):
    total = []
    for o in range(2):
        rows = (keep_ref[o] + other_ref[o].astype(F32)).astype(BF16)
        total.append(dot(rows, place_ref[...], (0, 0)))
    r, c = iota((64, 64), 0), iota((64, 64), 1)
    weave = (c == r % 2 * 32 + r // 2).astype(BF16)
    for ym in range(YM):
        halves = []
        for o in range(2):
            parts = [total[o][t * 32 : (t + 1) * 32, ym * 72 : (ym + 1) * 72] for t in range(8)]
            parts.append(jnp.zeros((32, 64), F32))
            halves.append(jnp.concatenate(parts, axis=1))
        pair = jnp.concatenate(halves, axis=0).astype(BF16)
        out_ref[ym * 64 : (ym + 1) * 64, :] = dot(weave, pair, (1, 0)).astype(BF16)


def join(keep, other, place):
    return pl.pallas_call(
        join_kernel,
        out_shape=jax.ShapeDtypeStruct((256, 640), BF16),
        compiler_params=PARAMS,
        name="join",
    )(keep, other, place)


def finish_kernel(x_ref, info_ref, pick_ref, cos_ref, sin_ref, vort_ref, out_hbm, out_ref, sems):
    x = x_ref[...].astype(F32)
    x = jnp.concatenate([x, x * info_ref[:, 2:3]], axis=0)
    lat = []
    for k in range(2):
        turned_x = jnp.concatenate([x[:, 12:], x[:, :12]], axis=1) if k else x
        rows = dot(pick_ref[...], turned_x.astype(BF16), (1, 1)).astype(BF16)
        lat.append(jnp.concatenate([rows[:, :256], rows[:, 256:]], axis=0))
    half = cos_ref.shape[1]
    copies = []
    for at in range(0, half, WIDTH):
        flow = dot(lat[0], cos_ref[:, at : at + WIDTH], (1, 0))
        flow += dot(lat[1], sin_ref[:, at : at + WIDTH], (1, 0))
        for h in range(2):
            span = slice(h * half + at, h * half + at + WIDTH)
            u = [flow[h * 288 + c * 96 : h * 288 + (c + 1) * 96] for c in range(3)]
            w = [vort_ref[c, :, span].astype(F32) for c in range(3)]
            for c in range(3):
                a, b = (c + 1) % 3, (c + 2) % 3
                out_ref[c, :, span] = (u[a] * w[b] - u[b] * w[a]).astype(BF16)
            part = pl.ds(h * half + at, WIDTH)
            copies.append(
                pltpu.make_async_copy(
                    out_ref.at[:, :, part], out_hbm.at[:, :, part], sems.at[len(copies)]
                )
            )
            copies[-1].start()
    for copy in copies:
        copy.wait()


def finish(rows, info, pick, cos, sin, vorticity):
    return pl.pallas_call(
        finish_kernel,
        out_shape=jax.ShapeDtypeStruct(vorticity.shape, BF16),
        out_specs=pl.BlockSpec(memory_space=pl.ANY),
        scratch_shapes=[
            pltpu.VMEM(vorticity.shape, BF16),
            pltpu.SemaphoreType.DMA((vorticity.shape[2] // WIDTH,)),
        ],
        compiler_params=PARAMS,
        name="finish",
    )(rows, info, pick, cos, sin, vorticity)


def shards(spectral, inverse, legendre, vorticity, degree_list, order_map):
    ym, core, mem = lax.axis_index("ym"), lax.axis_index("core"), lax.axis_index("mem")
    degrees = spectral.shape[0]
    packed = pack(
        spectral.reshape(degrees, 48, 192), inverse, jnp.transpose(legendre, (0, 2, 1))
    )
    received = lax.all_to_all(packed, ("ys", "ym"), 0, 0, tiled=True)
    where = jnp.stack([core, mem * 8 + ym * 2]).astype(jnp.int32)
    count = vorticity.shape[3]
    info, place, pick, cos, sin = tables(where, order_map, degree_list, count)
    keep, send = contract(received, info)
    other = lax.ppermute(send, "core", [(0, 1), (1, 0)])
    joined = join(keep, other, place)
    rows = lax.all_to_all(joined.reshape(128, 2, 640), ("ym", "mem"), 0, 0, tiled=True)

    field = jnp.transpose(vorticity, (0, 2, 1, 3)).reshape(3, 96, count)
    out = finish(rows.reshape(256, 640), info, pick, cos, sin, field)
    return jnp.transpose(out.reshape(3, 12, 8, count), (0, 2, 1, 3))


def solution(mesh):
    fine = Mesh(mesh.devices.reshape(YS, YM, CORES, 32), ("ys", "ym", "core", "mem"))
    grp = ("ys", "ym", "core")
    return jax.shard_map(
        shards,
        mesh=fine,
        in_specs=(
            P(grp, None, None, "mem", None),
            P(grp, None, None),
            P("mem", None, grp),
            P(None, "mem", grp, None),
            P(),
            P(),
        ),
        out_specs=P(None, "mem", grp, None),
        check_vma=False,
    )
```

```python
import math

import jax
import jax.numpy as jnp
from jax import lax
from jax.experimental import pallas as pl
from jax.experimental.pallas import tpu as pltpu
from jax.sharding import Mesh
from jax.sharding import PartitionSpec as P

YS, YM, CORES = 2, 4, 2
CHIPS = YS * YM
F32, BF16 = jnp.float32, jnp.bfloat16
STEPS = 4
WIDTH = 256
PARAMS = pltpu.CompilerParams(vmem_limit_bytes=16 << 20)


def dot(left, right, contract):
    return lax.dot_general(left, right, ((contract[:1], contract[1:]), ((), ())), preferred_element_type=F32)


def iota(shape, axis):
    return lax.broadcasted_iota(jnp.int32, shape, axis)


def pack_kernel(
    spec_hbm, inv_hbm, leg_hbm, out_hbm, out_ref, spec_ref, inv_ref, leg_ref, solved_ref, sems, out_sems
):
    degrees = spec_ref.shape[0]
    rows = degrees * 8
    step = degrees // STEPS
    copies = [pltpu.make_async_copy(leg_hbm, leg_ref, sems.at[2 * STEPS])]
    for i in range(STEPS):
        cut = pl.ds(i * step, step)
        copies.append(pltpu.make_async_copy(inv_hbm.at[cut], inv_ref.at[cut], sems.at[2 * i]))
        copies.append(pltpu.make_async_copy(spec_hbm.at[cut], spec_ref.at[cut], sems.at[2 * i + 1]))
    for copy in copies:
        copy.start()
    r, c = iota((256, 256), 0), iota((256, 256), 1)
    turn = (r == c % 32 * 8 + c // 32).astype(BF16)
    swap = (c == r % degrees * 8 + r // degrees).astype(BF16)
    r, c = iota((192, 192), 0), iota((192, 192), 1)
    side = (r // 12 % 2 != lax.axis_index("core")).astype(jnp.int32)
    near = (c == r // 96 * 96 + side * 48 + r % 96 // 24 * 12 + r % 12).astype(F32).astype(BF16)
    copies[0].wait()
    table = dot(leg_ref[...].reshape(rows, 256), turn, (1, 0)).astype(BF16)
    for chip in range(CHIPS):
        for o in range(2):
            at = (chip % YM * 2 + o) * degrees
            out_ref[chip, :, o * 256 : (o + 1) * 256] = table[at : at + degrees, :]
    for i in range(STEPS):
        copies[2 * i + 1].wait()
        copies[2 * i + 2].wait()
        for l in range(i * step, (i + 1) * step):
            product = dot(spec_ref[l], inv_ref[l], (1, 1))
            for ck in range(6):
                solved_ref[ck, l * 8 : (l + 1) * 8, :] = product[ck * 8 : (ck + 1) * 8, :]
    by_order = [dot(swap, solved_ref[ck].astype(BF16), (1, 0)).astype(BF16) for ck in range(6)]
    by_order = [dot(v, near, (1, 0)) for v in by_order]
    half = by_order[0].shape[1] // YS
    sends = []
    for ys in range(YS):
        for ym in range(YM):
            parts = []
            for o in range(2):
                at = (ym * 2 + o) * degrees
                parts += [v[at : at + degrees, ys * half : (ys + 1) * half] for v in by_order]
            chip = ys * YM + ym
            out_ref[chip, :, 512:] = jnp.concatenate(parts, axis=1).astype(BF16)
            sends.append(pltpu.make_async_copy(out_ref.at[chip], out_hbm.at[chip], out_sems.at[chip]))
            sends[-1].start()
    for send in sends:
        send.wait()


def pack(spectral, inverse, legendre):
    degrees = spectral.shape[0]
    return pl.pallas_call(
        pack_kernel,
        out_shape=jax.ShapeDtypeStruct((CHIPS, degrees, 1664), BF16),
        in_specs=[pl.BlockSpec(memory_space=pl.ANY)] * 3,
        out_specs=pl.BlockSpec(memory_space=pl.ANY),
        scratch_shapes=[
            pltpu.VMEM((CHIPS, degrees, 1664), BF16),
            pltpu.VMEM(spectral.shape, BF16),
            pltpu.VMEM(inverse.shape, BF16),
            pltpu.VMEM(legendre.shape, BF16),
            pltpu.VMEM((6, degrees * 8, 192), F32),
            pltpu.SemaphoreType.DMA((2 * STEPS + 1,)),
            pltpu.SemaphoreType.DMA((CHIPS,)),
        ],
        compiler_params=pltpu.CompilerParams(vmem_limit_bytes=60 << 20),
        name="pack",
    )(spectral, inverse, legendre)


def turned(values, index):
    hit = iota(index.shape, 1) == index
    return jnp.sum(jnp.where(hit, values, 0), axis=1, keepdims=True)


def tables_kernel(where_ref, order_ref, degree_ref, info_ref, place_ref, pick_ref, cos_ref, sin_ref):
    core, first = where_ref[0], where_ref[1]
    r = iota((256, 512), 0)
    own = turned(degree_ref[...].astype(F32), r // 32 * 64 + core * 32 + r % 32)
    orders = order_ref[...].astype(F32)
    for o in range(2):
        order = turned(orders, jnp.full((256, 256), first + o, jnp.int32))
        info_ref[:, o : o + 1] = (own >= order).astype(F32)
    q, col = iota((288, 384), 0), iota((288, 384), 1)
    hit = col == q % 48 // 12 * 72 + q // 48 * 12 + q % 12
    place_ref[...] = hit.astype(F32).astype(BF16)
    row, col = iota((288, 640), 0), iota((288, 640), 1)
    hit = col == row % 8 * 72 + row // 96 * 24 + row // 8 % 12
    pick_ref[...] = hit.astype(F32).astype(BF16)
    r = iota((256, 256), 0)
    order = turned(orders, r % 64 // 2 * 8 + r // 64 * 2 + r % 2)
    weight = jnp.where(order == 0, 1.0, 2.0)
    info_ref[:, 2:3] = 1.0 - 2.0 * (order - 2.0 * jnp.floor(order * 0.5))
    half = cos_ref.shape[1]
    count = 2 * half
    for at in range(0, half, 128):
        product = order * (iota((256, 128), 1) + at).astype(F32)
        phase = product - jnp.floor(product * (1.0 / count)) * count
        phase = jnp.where(phase < 0, phase + count, phase)
        phase = jnp.where(phase >= count, phase - count, phase)
        angle = phase * (2.0 * math.pi / count)
        cos_ref[:, at : at + 128] = (weight * jnp.cos(angle)).astype(BF16)
        sin_ref[:, at : at + 128] = (-weight * jnp.sin(angle)).astype(BF16)


def tables(where, order_map, degree_list, count):
    return pl.pallas_call(
        tables_kernel,
        out_shape=(
            jax.ShapeDtypeStruct((256, 3), F32),
            jax.ShapeDtypeStruct((288, 384), BF16),
            jax.ShapeDtypeStruct((288, 640), BF16),
            jax.ShapeDtypeStruct((256, count // 2), BF16),
            jax.ShapeDtypeStruct((256, count // 2), BF16),
        ),
        in_specs=[pl.BlockSpec(memory_space=pltpu.SMEM)]
        + [pl.BlockSpec(memory_space=pltpu.VMEM)] * 2,
        compiler_params=PARAMS,
        name="tables",
    )(where, order_map[None, :], degree_list[None, :])


def contract_kernel(x_ref, info_ref, keep_ref, send_ref):
    for o in range(2):
        table = x_ref[:, :, o * 256 : (o + 1) * 256].reshape(256, 256)
        table = jnp.where(info_ref[:, o : o + 1] > 0, table, jnp.zeros((), BF16))
        radial = x_ref[:, :, 512 + o * 512 : 1152 + o * 512].reshape(256, 640)
        partial = dot(radial, table, (0, 0))
        for ck in range(6):
            at = o * 64 + ck * 96
            keep_ref[o, ck * 48 : (ck + 1) * 48, :] = partial[at : at + 48, :]
            send_ref[o, ck * 48 : (ck + 1) * 48, :] = partial[at + 48 : at + 96, :]


def contract(received, info):
    return pl.pallas_call(
        contract_kernel,
        out_shape=(
            jax.ShapeDtypeStruct((2, 288, 256), F32),
            jax.ShapeDtypeStruct((2, 288, 256), F32),
        ),
        compiler_params=PARAMS,
        name="contract",
    )(received, info)


def join_kernel(keep_ref, other_ref, place_ref, out_ref):
    total = []
    for o in range(2):
        rows = (keep_ref[o] + other_ref[o]).astype(BF16)
        total.append(dot(rows, place_ref[...], (0, 0)))
    r, c = iota((64, 64), 0), iota((64, 64), 1)
    weave = (c == r % 2 * 32 + r // 2).astype(BF16)
    for ym in range(YM):
        halves = []
        for o in range(2):
            parts = [total[o][t * 32 : (t + 1) * 32, ym * 72 : (ym + 1) * 72] for t in range(8)]
            parts.append(jnp.zeros((32, 64), F32))
            halves.append(jnp.concatenate(parts, axis=1))
        pair = jnp.concatenate(halves, axis=0).astype(BF16)
        out_ref[ym * 64 : (ym + 1) * 64, :] = dot(weave, pair, (1, 0)).astype(BF16)


def join(keep, other, place):
    return pl.pallas_call(
        join_kernel,
        out_shape=jax.ShapeDtypeStruct((256, 640), BF16),
        compiler_params=PARAMS,
        name="join",
    )(keep, other, place)


def finish_kernel(x_ref, info_ref, pick_ref, cos_ref, sin_ref, vort_ref, out_hbm, out_ref, sems):
    x = x_ref[...].astype(F32)
    x = jnp.concatenate([x, x * info_ref[:, 2:3]], axis=0)
    lat = []
    for k in range(2):
        turned_x = jnp.concatenate([x[:, 12:], x[:, :12]], axis=1) if k else x
        rows = dot(pick_ref[...], turned_x.astype(BF16), (1, 1)).astype(BF16)
        lat.append(jnp.concatenate([rows[:, :256], rows[:, 256:]], axis=0))
    half = cos_ref.shape[1]
    copies = []
    for at in range(0, half, WIDTH):
        flow = dot(lat[0], cos_ref[:, at : at + WIDTH], (1, 0))
        flow += dot(lat[1], sin_ref[:, at : at + WIDTH], (1, 0))
        for h in range(2):
            span = slice(h * half + at, h * half + at + WIDTH)
            u = [flow[h * 288 + c * 96 : h * 288 + (c + 1) * 96] for c in range(3)]
            w = [vort_ref[c, :, span].astype(F32) for c in range(3)]
            for c in range(3):
                a, b = (c + 1) % 3, (c + 2) % 3
                out_ref[c, :, span] = (u[a] * w[b] - u[b] * w[a]).astype(BF16)
            part = pl.ds(h * half + at, WIDTH)
            copies.append(
                pltpu.make_async_copy(
                    out_ref.at[:, :, part], out_hbm.at[:, :, part], sems.at[len(copies)]
                )
            )
            copies[-1].start()
    for copy in copies:
        copy.wait()


def finish(rows, info, pick, cos, sin, vorticity):
    return pl.pallas_call(
        finish_kernel,
        out_shape=jax.ShapeDtypeStruct(vorticity.shape, BF16),
        out_specs=pl.BlockSpec(memory_space=pl.ANY),
        scratch_shapes=[
            pltpu.VMEM(vorticity.shape, BF16),
            pltpu.SemaphoreType.DMA((vorticity.shape[2] // WIDTH,)),
        ],
        compiler_params=PARAMS,
        name="finish",
    )(rows, info, pick, cos, sin, vorticity)


def shards(spectral, inverse, legendre, vorticity, degree_list, order_map):
    ym, core, mem = lax.axis_index("ym"), lax.axis_index("core"), lax.axis_index("mem")
    degrees = spectral.shape[0]
    packed = pack(
        spectral.reshape(degrees, 48, 192), inverse, jnp.transpose(legendre, (0, 2, 1))
    )
    received = lax.all_to_all(packed, ("ys", "ym"), 0, 0, tiled=True)
    where = jnp.stack([core, mem * 8 + ym * 2]).astype(jnp.int32)
    count = vorticity.shape[3]
    info, place, pick, cos, sin = tables(where, order_map, degree_list, count)
    keep, send = contract(received, info)
    other = lax.ppermute(send, "core", [(0, 1), (1, 0)])
    joined = join(keep, other, place)
    rows = lax.all_to_all(joined.reshape(128, 2, 640), ("ym", "mem"), 0, 0, tiled=True)

    field = jnp.transpose(vorticity, (0, 2, 1, 3)).reshape(3, 96, count)
    out = finish(rows.reshape(256, 640), info, pick, cos, sin, field)
    return jnp.transpose(out.reshape(3, 12, 8, count), (0, 2, 1, 3))


def solution(mesh):
    fine = Mesh(mesh.devices.reshape(YS, YM, CORES, 32), ("ys", "ym", "core", "mem"))
    grp = ("ys", "ym", "core")
    return jax.shard_map(
        shards,
        mesh=fine,
        in_specs=(
            P(grp, None, None, "mem", None),
            P(grp, None, None),
            P("mem", None, grp),
            P(None, "mem", grp, None),
            P(),
            P(),
        ),
        out_specs=P(None, "mem", grp, None),
        check_vma=False,
    )
```

```python
import math

import jax
import jax.numpy as jnp
from jax import lax
from jax.experimental import pallas as pl
from jax.experimental.pallas import tpu as pltpu
from jax.sharding import Mesh
from jax.sharding import PartitionSpec as P

YS, YM, CORES = 2, 4, 2
CHIPS = YS * YM
F32, BF16 = jnp.float32, jnp.bfloat16
STEPS = 4
WIDTH = 384
PARAMS = pltpu.CompilerParams(vmem_limit_bytes=16 << 20)


def dot(left, right, contract):
    return lax.dot_general(left, right, ((contract[:1], contract[1:]), ((), ())), preferred_element_type=F32)


def iota(shape, axis):
    return lax.broadcasted_iota(jnp.int32, shape, axis)


def pack_kernel(
    spec_hbm, inv_hbm, leg_hbm, out_hbm, out_ref, spec_ref, inv_ref, leg_ref, solved_ref, sems, out_sems
):
    degrees = spec_ref.shape[0]
    rows = degrees * 8
    step = degrees // STEPS
    copies = [pltpu.make_async_copy(leg_hbm, leg_ref, sems.at[2 * STEPS])]
    for i in range(STEPS):
        cut = pl.ds(i * step, step)
        copies.append(pltpu.make_async_copy(inv_hbm.at[cut], inv_ref.at[cut], sems.at[2 * i]))
        copies.append(pltpu.make_async_copy(spec_hbm.at[cut], spec_ref.at[cut], sems.at[2 * i + 1]))
    for copy in copies:
        copy.start()
    r, c = iota((256, 256), 0), iota((256, 256), 1)
    turn = (r == c % 32 * 8 + c // 32).astype(BF16)
    swap = (c == r % degrees * 8 + r // degrees).astype(BF16)
    r, c = iota((192, 192), 0), iota((192, 192), 1)
    side = (r // 12 % 2 != lax.axis_index("core")).astype(jnp.int32)
    near = (c == r // 96 * 96 + side * 48 + r % 96 // 24 * 12 + r % 12).astype(F32).astype(BF16)
    copies[0].wait()
    table = dot(leg_ref[...].reshape(rows, 256), turn, (1, 0)).astype(BF16)
    for chip in range(CHIPS):
        for o in range(2):
            at = (chip % YM * 2 + o) * degrees
            out_ref[chip, :, o * 256 : (o + 1) * 256] = table[at : at + degrees, :]
    for i in range(STEPS):
        copies[2 * i + 1].wait()
        copies[2 * i + 2].wait()
        for l in range(i * step, (i + 1) * step):
            product = dot(spec_ref[l], inv_ref[l], (1, 1))
            for ck in range(6):
                solved_ref[ck, l * 8 : (l + 1) * 8, :] = product[ck * 8 : (ck + 1) * 8, :]
    by_order = [dot(swap, solved_ref[ck].astype(BF16), (1, 0)).astype(BF16) for ck in range(6)]
    by_order = [dot(v, near, (1, 0)) for v in by_order]
    half = by_order[0].shape[1] // YS
    sends = []
    for ys in range(YS):
        for ym in range(YM):
            parts = []
            for o in range(2):
                at = (ym * 2 + o) * degrees
                parts += [v[at : at + degrees, ys * half : (ys + 1) * half] for v in by_order]
            chip = ys * YM + ym
            out_ref[chip, :, 512:] = jnp.concatenate(parts, axis=1).astype(BF16)
            sends.append(pltpu.make_async_copy(out_ref.at[chip], out_hbm.at[chip], out_sems.at[chip]))
            sends[-1].start()
    for send in sends:
        send.wait()


def pack(spectral, inverse, legendre):
    degrees = spectral.shape[0]
    return pl.pallas_call(
        pack_kernel,
        out_shape=jax.ShapeDtypeStruct((CHIPS, degrees, 1664), BF16),
        in_specs=[pl.BlockSpec(memory_space=pl.ANY)] * 3,
        out_specs=pl.BlockSpec(memory_space=pl.ANY),
        scratch_shapes=[
            pltpu.VMEM((CHIPS, degrees, 1664), BF16),
            pltpu.VMEM(spectral.shape, BF16),
            pltpu.VMEM(inverse.shape, BF16),
            pltpu.VMEM(legendre.shape, BF16),
            pltpu.VMEM((6, degrees * 8, 192), F32),
            pltpu.SemaphoreType.DMA((2 * STEPS + 1,)),
            pltpu.SemaphoreType.DMA((CHIPS,)),
        ],
        compiler_params=pltpu.CompilerParams(vmem_limit_bytes=60 << 20),
        name="pack",
    )(spectral, inverse, legendre)


def turned(values, index):
    hit = iota(index.shape, 1) == index
    return jnp.sum(jnp.where(hit, values, 0), axis=1, keepdims=True)


def tables_kernel(where_ref, order_ref, degree_ref, info_ref, place_ref, pick_ref, cos_ref, sin_ref):
    core, first = where_ref[0], where_ref[1]
    r = iota((256, 512), 0)
    own = turned(degree_ref[...].astype(F32), r // 32 * 64 + core * 32 + r % 32)
    orders = order_ref[...].astype(F32)
    for o in range(2):
        order = turned(orders, jnp.full((256, 256), first + o, jnp.int32))
        info_ref[:, o : o + 1] = (own >= order).astype(F32)
    q, col = iota((288, 384), 0), iota((288, 384), 1)
    hit = col == q % 48 // 12 * 72 + q // 48 * 12 + q % 12
    place_ref[...] = hit.astype(F32).astype(BF16)
    row, col = iota((288, 640), 0), iota((288, 640), 1)
    hit = col == row % 8 * 72 + row // 96 * 24 + row // 8 % 12
    pick_ref[...] = hit.astype(F32).astype(BF16)
    r = iota((256, 256), 0)
    order = turned(orders, r % 64 // 2 * 8 + r // 64 * 2 + r % 2)
    weight = jnp.where(order == 0, 1.0, 2.0)
    info_ref[:, 2:3] = 1.0 - 2.0 * (order - 2.0 * jnp.floor(order * 0.5))
    half = cos_ref.shape[1]
    count = 2 * half
    for at in range(0, half, 128):
        product = order * (iota((256, 128), 1) + at).astype(F32)
        phase = product - jnp.floor(product * (1.0 / count)) * count
        phase = jnp.where(phase < 0, phase + count, phase)
        phase = jnp.where(phase >= count, phase - count, phase)
        angle = phase * (2.0 * math.pi / count)
        cos_ref[:, at : at + 128] = (weight * jnp.cos(angle)).astype(BF16)
        sin_ref[:, at : at + 128] = (-weight * jnp.sin(angle)).astype(BF16)


def tables(where, order_map, degree_list, count):
    return pl.pallas_call(
        tables_kernel,
        out_shape=(
            jax.ShapeDtypeStruct((256, 3), F32),
            jax.ShapeDtypeStruct((288, 384), BF16),
            jax.ShapeDtypeStruct((288, 640), BF16),
            jax.ShapeDtypeStruct((256, count // 2), BF16),
            jax.ShapeDtypeStruct((256, count // 2), BF16),
        ),
        in_specs=[pl.BlockSpec(memory_space=pltpu.SMEM)]
        + [pl.BlockSpec(memory_space=pltpu.VMEM)] * 2,
        compiler_params=PARAMS,
        name="tables",
    )(where, order_map[None, :], degree_list[None, :])


def contract_kernel(x_ref, info_ref, keep_ref, send_ref):
    for o in range(2):
        table = x_ref[:, :, o * 256 : (o + 1) * 256].reshape(256, 256)
        table = jnp.where(info_ref[:, o : o + 1] > 0, table, jnp.zeros((), BF16))
        radial = x_ref[:, :, 512 + o * 512 : 1152 + o * 512].reshape(256, 640)
        partial = dot(radial, table, (0, 0))
        for ck in range(6):
            at = o * 64 + ck * 96
            keep_ref[o, ck * 48 : (ck + 1) * 48, :] = partial[at : at + 48, :]
            send_ref[o, ck * 48 : (ck + 1) * 48, :] = partial[at + 48 : at + 96, :].astype(BF16)


def contract(received, info):
    return pl.pallas_call(
        contract_kernel,
        out_shape=(
            jax.ShapeDtypeStruct((2, 288, 256), F32),
            jax.ShapeDtypeStruct((2, 288, 256), BF16),
        ),
        compiler_params=PARAMS,
        name="contract",
    )(received, info)


def join_kernel(keep_ref, other_ref, place_ref, out_ref):
    total = []
    for o in range(2):
        rows = (keep_ref[o] + other_ref[o].astype(F32)).astype(BF16)
        total.append(dot(rows, place_ref[...], (0, 0)))
    r, c = iota((64, 64), 0), iota((64, 64), 1)
    weave = (c == r % 2 * 32 + r // 2).astype(BF16)
    for ym in range(YM):
        halves = []
        for o in range(2):
            parts = [total[o][t * 32 : (t + 1) * 32, ym * 72 : (ym + 1) * 72] for t in range(8)]
            parts.append(jnp.zeros((32, 64), F32))
            halves.append(jnp.concatenate(parts, axis=1))
        pair = jnp.concatenate(halves, axis=0).astype(BF16)
        out_ref[ym * 64 : (ym + 1) * 64, :] = dot(weave, pair, (1, 0)).astype(BF16)


def join(keep, other, place):
    return pl.pallas_call(
        join_kernel,
        out_shape=jax.ShapeDtypeStruct((256, 640), BF16),
        compiler_params=PARAMS,
        name="join",
    )(keep, other, place)


def finish_kernel(x_ref, info_ref, pick_ref, cos_ref, sin_ref, vort_ref, out_hbm, out_ref, sems):
    x = x_ref[...].astype(F32)
    x = jnp.concatenate([x, x * info_ref[:, 2:3]], axis=0)
    lat = []
    for k in range(2):
        turned_x = jnp.concatenate([x[:, 12:], x[:, :12]], axis=1) if k else x
        rows = dot(pick_ref[...], turned_x.astype(BF16), (1, 1)).astype(BF16)
        lat.append(jnp.concatenate([rows[:, :256], rows[:, 256:]], axis=0))
    half = cos_ref.shape[1]
    copies = []
    for at in range(0, half, WIDTH):
        flow = dot(lat[0], cos_ref[:, at : at + WIDTH], (1, 0))
        flow += dot(lat[1], sin_ref[:, at : at + WIDTH], (1, 0))
        for h in range(2):
            span = slice(h * half + at, h * half + at + WIDTH)
            u = [flow[h * 288 + c * 96 : h * 288 + (c + 1) * 96] for c in range(3)]
            w = [vort_ref[c, :, span].astype(F32) for c in range(3)]
            for c in range(3):
                a, b = (c + 1) % 3, (c + 2) % 3
                out_ref[c, :, span] = (u[a] * w[b] - u[b] * w[a]).astype(BF16)
            part = pl.ds(h * half + at, WIDTH)
            copies.append(
                pltpu.make_async_copy(
                    out_ref.at[:, :, part], out_hbm.at[:, :, part], sems.at[len(copies)]
                )
            )
            copies[-1].start()
    for copy in copies:
        copy.wait()


def finish(rows, info, pick, cos, sin, vorticity):
    return pl.pallas_call(
        finish_kernel,
        out_shape=jax.ShapeDtypeStruct(vorticity.shape, BF16),
        out_specs=pl.BlockSpec(memory_space=pl.ANY),
        scratch_shapes=[
            pltpu.VMEM(vorticity.shape, BF16),
            pltpu.SemaphoreType.DMA((vorticity.shape[2] // WIDTH,)),
        ],
        compiler_params=PARAMS,
        name="finish",
    )(rows, info, pick, cos, sin, vorticity)


def shards(spectral, inverse, legendre, vorticity, degree_list, order_map):
    ym, core, mem = lax.axis_index("ym"), lax.axis_index("core"), lax.axis_index("mem")
    degrees = spectral.shape[0]
    packed = pack(
        spectral.reshape(degrees, 48, 192), inverse, jnp.transpose(legendre, (0, 2, 1))
    )
    received = lax.all_to_all(packed, ("ys", "ym"), 0, 0, tiled=True)
    where = jnp.stack([core, mem * 8 + ym * 2]).astype(jnp.int32)
    count = vorticity.shape[3]
    info, place, pick, cos, sin = tables(where, order_map, degree_list, count)
    keep, send = contract(received, info)
    other = lax.ppermute(send, "core", [(0, 1), (1, 0)])
    joined = join(keep, other, place)
    rows = lax.all_to_all(joined.reshape(128, 2, 640), ("ym", "mem"), 0, 0, tiled=True)

    field = jnp.transpose(vorticity, (0, 2, 1, 3)).reshape(3, 96, count)
    out = finish(rows.reshape(256, 640), info, pick, cos, sin, field)
    return jnp.transpose(out.reshape(3, 12, 8, count), (0, 2, 1, 3))


def solution(mesh):
    fine = Mesh(mesh.devices.reshape(YS, YM, CORES, 32), ("ys", "ym", "core", "mem"))
    grp = ("ys", "ym", "core")
    return jax.shard_map(
        shards,
        mesh=fine,
        in_specs=(
            P(grp, None, None, "mem", None),
            P(grp, None, None),
            P("mem", None, grp),
            P(None, "mem", grp, None),
            P(),
            P(),
        ),
        out_specs=P(None, "mem", grp, None),
        check_vma=False,
    )
```
